32 devices in a mesh: dp: 8 (over y, x, core), hid: 4 (over z).
Axes of the slice: x: 2, y: 2, z: 4, core: 2. Of those that a mesh axis runs over, the one named last changes fastest.
Arguments:
- tokens: bfloat16 [8, 1024, 768], P('dp', 'hid'), may hold values from -6 to 6
- cotangent: bfloat16 [8, 1024, 768], P('dp', 'hid'), may hold values from -6 to 6
- item_lengths: int32 [8], P('dp'), may hold values from 256 to 1024, as said below
- time_steps: int32 [8], P('dp'), may hold values from 0 to 999
- class_labels: int32 [8], P('dp'), may hold values from 0 to 999
- routes: int32 [8, 1024, 2], P('dp'), may hold values from 0 to 7, all different within a row; in each aligned block of 1024 rows (0 to 1023, 1024 to 2047, ..., all dimensions but the last counted through in order) at most 320 rows name the same one
- time_table: bfloat16 [1000, 768], P('hid'), may hold values from -6 to 6
- class_table: bfloat16 [1000, 768], P('hid'), may hold values from -6 to 6
- modulation: bfloat16 [768, 4608], P('hid'), may hold values from -0.21875 to 0.21875
- qkv_weight: bfloat16 [768, 2304], P('hid'), may hold values from -0.21875 to 0.21875
- out_weight: bfloat16 [768, 768], P('hid'), may hold values from -1.5 to 1.5
- router: bfloat16 [768, 8], P('hid'), may hold values from -0.119628906 to 0.119628906
- shared_up: bfloat16 [768, 3072], P(None, 'hid'), may hold values from -0.21875 to 0.21875
- shared_down: bfloat16 [3072, 768], P('hid'), may hold values from -0.109375 to 0.109375
- expert_up: bfloat16 [8, 768, 3072], P('dp', None, 'hid'), may hold values from -0.21875 to 0.21875
- expert_down: bfloat16 [8, 3072, 768], P('dp', 'hid'), may hold values from -0.109375 to 0.109375
Outputs:
- output: bfloat16 [8, 1024, 768], P('dp', 'hid')
- tokens_grad: float32 [8, 1024, 768], P('dp', 'hid')
- time_table_grad: float32 [1000, 768], P('hid')
- class_table_grad: float32 [1000, 768], P('hid')
- modulation_grad: float32 [768, 4608], P('hid')
- qkv_weight_grad: float32 [768, 2304], P('hid')
- out_weight_grad: float32 [768, 768], P('hid')
- router_grad: float32 [768, 8], P('hid')
- shared_up_grad: float32 [768, 3072], P(None, 'hid')
- shared_down_grad: float32 [3072, 768], P('hid')
- expert_up_grad: float32 [8, 768, 3072], P('dp', None, 'hid')
- expert_down_grad: float32 [8, 3072, 768], P('dp', 'hid')
The draws below stay inside these ranges and needn't reach their ends.
Inputs may be any that keep to these rules, and one draw needn't show every extreme that they name: `routes`: the 2 experts of a patch differ. Among the patches of the 1 items of one index of dp, no expert is named by more than 320 patches, and in some index of dp some expert is named by exactly 320. `item_lengths`: each item has 256 or 1024 valid patches at its front; the rest are padding, which is never a key.
All inputs are finite; a program needn't handle non-finite values.
Results may differ from the reference program's by a relative error of at most 0.023.
Values may be sent and summed in bfloat16 or wider, within the bound.
No kernel may reach another device: no remote copies, remote signals or barrier semaphores. Data moves between devices by JAX's collectives and lax.ppermute only.
A program may use at most 256 MiB of HBM per device.

```python
import math
from functools import partial
import jax
import jax.numpy as jnp
import numpy as np
from jax import lax

D = 768
HEADS = 12
HDIM = 64
FF = 3072
STEPS = 1000
CLASSES = 1000
TOP = 2
LEN = 1024
IG = 1
EXPERTS = 8
ITEMS = 8
CAP = 320
N_DP = 8


def draw_item_lengths(key, part):
    full_flags = jax.random.randint(key, (ITEMS,), 0, 2)
    full_flags = full_flags.at[0].set(1).at[1].set(0)
    return jnp.where(full_flags == 1, LEN, LEN // 4).astype(jnp.int32)


def plant(values, key, low, largest):
    dims = values.shape
    index_at = [jax.random.randint(jax.random.fold_in(key, axis), (), 0, dims[axis]) for axis in range(len(dims))]
    values = values.at[tuple(index_at)].set(low)
    longest = dims.index(max(dims))
    index_at[longest] = (index_at[longest] + 1) % dims[longest]
    return values.at[tuple(index_at)].set(largest)


def levels(rng, dims, shards, least, top_value):
    level, own = 1.0, jax.random.fold_in(rng, 6)
    for axis_at, parts in shards:
        heights = jnp.exp(jax.random.uniform(jax.random.fold_in(own, axis_at), (parts,), jnp.float32, least / len(shards), top_value / len(shards)))
        level = level * jnp.repeat(heights, dims[axis_at] // parts).reshape([-1 if axis == axis_at else 1 for axis in range(len(dims))])
    return level


def assign_block(rng, own, number, rows, number_of, top, most, lean):
    ranking = jax.random.permutation(rng, number_of)
    packed, ordinary = load_shares(number_of, rows * top, most, lean, True), load_shares(number_of, rows * top, most, lean, False)
    places = jnp.arange(number_of)

    def named(lengths, rotation):
        used = int((lengths > 0).sum())
        fixed = max(1, used // 4)
        shifted = fixed + (places - fixed + rotation * (used - fixed)) % max(1, number_of - fixed)
        return jnp.zeros((number_of,), jnp.int32).at[ranking[jnp.where(places < fixed, places, shifted)]].set(jnp.asarray(lengths, jnp.int32))

    lengths = jnp.where(number % 4 == 0, named(packed, number // 4), named(ordinary, number - number // 4 - 1))
    mixed = jax.random.permutation(jax.random.fold_in(own, 3), number_of)
    source_of, sink = mixed[0:number_of // 2 * 2:2], mixed[1:number_of // 2 * 2:2]
    room = jnp.minimum(lengths[source_of] - 1, most - lengths[sink]) // 2
    room = jnp.where((source_of == ranking[0]) | (sink == ranking[0]) | (lengths[sink] == 0), 0, jnp.maximum(room, 0))
    shifted = jax.random.randint(jax.random.fold_in(own, 4), (number_of // 2,), 0, 1 << 20) % (room + 1)
    lengths = lengths.at[source_of].add(-shifted).at[sink].add(shifted)
    items = jnp.searchsorted(jnp.cumsum(lengths), jnp.arange(rows * top), side="right").astype(jnp.int32)
    listing = items.reshape(top, rows).T
    listing = listing[jax.random.permutation(jax.random.fold_in(own, 1), rows)]
    rotation = jax.random.randint(jax.random.fold_in(own, 2), (rows, 1), 0, top)
    return jnp.take_along_axis(listing, (jnp.arange(top)[None, :] + rotation) % top, axis=1)


def load_shares(number_of, total, reach, slope, full):
    loads = [(1 << 20) // math.isqrt(standing ** slope) + 1 for standing in range(1, number_of + 1)]
    largest = reach if full else min(reach, max(-(-total // number_of), total * loads[0] // sum(loads)))
    least = 1 if total - largest >= number_of - 1 else 0
    holding, spare = [largest] + [least] * (number_of - 1), total - largest - least * (number_of - 1)
    while spare > 0:
        movable = [i for i in range(1, number_of) if holding[i] < largest] or [i for i in range(1, number_of) if holding[i] < reach]
        mass, left = sum([loads[i] for i in movable]), spare
        for i in movable:
            more = min(reach - holding[i], max(1, left * loads[i] // mass), spare)
            holding[i] = holding[i] + more
            spare = spare - more
    return np.array(holding)


def gaussian(own_key, dims, deviation, most, pieces=(), kind=jnp.bfloat16):
    values = deviation * jax.random.normal(own_key, dims, jnp.float32)
    if pieces:
        values = values * levels(own_key, dims, pieces, -0.22, 0.18)
    return jnp.clip(values, -most, most).astype(kind)


def setup_inputs(seed: int = 0) -> dict:
    streams_of = jax.random.split(jax.random.key(seed), 17)
    tokens = gaussian(streams_of[0], (ITEMS, LEN, D), 1.0, 6.0, ((0, 8), (1, 4)))
    cotangent = gaussian(streams_of[1], (ITEMS, LEN, D), 1.0, 6.0, ((0, 8), (1, 4)))
    item_lengths = draw_item_lengths(jax.random.fold_in(streams_of[16], 71), 0)
    time_steps = plant(jax.random.randint(streams_of[3], (ITEMS,), 0, STEPS), jax.random.fold_in(streams_of[3], 1), 0, STEPS - 1).astype(jnp.int32)
    class_labels = plant(jax.random.randint(streams_of[4], (ITEMS,), 0, CLASSES), jax.random.fold_in(streams_of[4], 1), 0, CLASSES - 1).astype(jnp.int32)
    routes_keys = jax.random.split(jax.random.fold_in(streams_of[5], 1), ITEMS * LEN // (IG * LEN))
    routes_turns = jax.random.permutation(jax.random.fold_in(streams_of[5], 3), ITEMS * LEN // (IG * LEN))
    routes = jax.vmap(lambda own, number: assign_block(jax.random.fold_in(streams_of[5], 2), own, number, IG * LEN, EXPERTS, TOP, CAP, 1))(routes_keys, routes_turns).reshape((ITEMS, LEN, TOP))
    time_table = gaussian(streams_of[6], (STEPS, D), 1.0, 6.0, ((0, 4),))
    class_table = gaussian(streams_of[7], (CLASSES, D), 1.0, 6.0, ((0, 4),))
    modulation = gaussian(streams_of[8], (D, 6 * D), D ** -0.5, 0.21875, ((0, 4),))
    qkv_weight = gaussian(streams_of[9], (D, 3 * D), D ** -0.5, 0.21875, ((0, 4),))
    out_weight = gaussian(streams_of[10], (D, D), 16 ** -0.5, 1.5, ((0, 4),))
    router = gaussian(streams_of[11], (D, EXPERTS), 0.02, 0.119628906, ((0, 4),))
    shared_up = gaussian(streams_of[12], (D, FF), D ** -0.5, 0.21875, ((1, 4),))
    shared_down = gaussian(streams_of[13], (FF, D), FF ** -0.5, 0.109375, ((0, 4),))
    expert_up = gaussian(streams_of[14], (EXPERTS, D, FF), D ** -0.5, 0.21875, ((0, 8), (2, 4)))
    expert_down = gaussian(streams_of[15], (EXPERTS, FF, D), FF ** -0.5, 0.109375, ((0, 8), (1, 4)))
    return dict(tokens=tokens, cotangent=cotangent, item_lengths=item_lengths, time_steps=time_steps, class_labels=class_labels, routes=routes, time_table=time_table, class_table=class_table, modulation=modulation, qkv_weight=qkv_weight, out_weight=out_weight, router=router, shared_up=shared_up, shared_down=shared_down, expert_up=expert_up, expert_down=expert_down)


@jax.custom_vjp
def low(v):
    return lax.optimization_barrier(v.astype(jnp.bfloat16)).astype(jnp.float32)

@jax.custom_vjp
def low_back(v):
    return v

def low_keep(v):
    return (low(v), None)

def low_pass(kept, grad):
    return (grad,)

def back_keep(v):
    return (v, None)

def back_low(kept, grad):
    return (low(grad),)
low.defvjp(low_keep, low_pass)
low_back.defvjp(back_keep, back_low)

def exact_dot(left, right):
    return jnp.dot(left, right, precision=lax.Precision.HIGHEST, preferred_element_type=jnp.float32)

def layer_norm(values):
    center = values - lax.optimization_barrier(jnp.mean(values, axis=-1, keepdims=True))
    return center * lax.rsqrt(lax.optimization_barrier(jnp.mean(center * center, axis=-1, keepdims=True)) + 1e-06)

def gelu_tanh(values):
    return 0.5 * values * (1.0 + jnp.tanh(0.7978845608028654 * (values + 0.044715 * values * values * values)))

def item_block(weights, item_args):
    qkv_f, out_f, router_f, up_f, down_f = weights
    patches, shifts, length = item_args
    normed = layer_norm(patches)
    hidden_in = low(normed * (1.0 + shifts[1]) + shifts[0])
    projected = low(low_back(exact_dot(hidden_in, qkv_f)))
    queries = projected[:, :D].reshape(LEN, HEADS, HDIM)
    key_rows = projected[:, D:2 * D].reshape(LEN, HEADS, HDIM)
    value_rows = projected[:, 2 * D:].reshape(LEN, HEADS, HDIM)
    scores = jnp.einsum('qhd,khd->hqk', queries, key_rows, precision=lax.Precision.HIGHEST) * HDIM ** (-0.5)
    valid_keys = jnp.arange(LEN, dtype=jnp.int32) < length
    scores = low_back(jnp.where(valid_keys[None, None, :], scores, -1e+30))
    top_score = lax.optimization_barrier(jnp.max(scores, axis=-1, keepdims=True))
    log_total = top_score + jnp.log(lax.optimization_barrier(jnp.sum(jnp.exp(scores - top_score), axis=-1, keepdims=True)))
    soft_low = low(jnp.exp(scores - log_total))
    head_mix = jnp.einsum('hqk,khd->qhd', soft_low, value_rows, precision=lax.Precision.HIGHEST)
    attended = low(low_back(head_mix.reshape(LEN, D)))
    branch = low_back(exact_dot(attended, out_f))
    residual = patches + shifts[2] * branch
    hidden_mid = low(layer_norm(residual) * (1.0 + shifts[4]) + shifts[3])
    logits = low_back(exact_dot(hidden_mid, router_f))
    shared_act = low(gelu_tanh(low_back(exact_dot(hidden_mid, up_f))))
    shared_out = exact_dot(shared_act, down_f)
    return (residual, hidden_mid, logits, shared_out)

def expert_rows(rows_pad, gates_pad, up_one, down_one, pair_ids):
    gathered = jnp.take(rows_pad, pair_ids // TOP, axis=0)
    gate_col = jnp.take(gates_pad, pair_ids)[:, None]
    pre_act = low_back(exact_dot(gathered, up_one))
    activated = low(gate_col * gelu_tanh(pre_act))
    return exact_dot(activated, down_one)

def reference(tokens, cotangent, item_lengths, time_steps, class_labels, routes, time_table, class_table, modulation, qkv_weight, out_weight, router, shared_up, shared_down, expert_up, expert_down):
    group_pairs = routes.reshape(N_DP, IG * LEN * TOP).astype(jnp.int32)
    expert_ids = jnp.arange(EXPERTS, dtype=jnp.int32)
    one_hot = (group_pairs[:, :, None] == expert_ids[None, None, :]).astype(jnp.int32)
    slot_of = (lax.optimization_barrier(jnp.sum(jnp.cumsum(one_hot, axis=1) * one_hot, axis=-1)) - 1).astype(jnp.int32)
    group_ids = jnp.arange(N_DP, dtype=jnp.int32)[:, None]
    target = (group_pairs * (N_DP * CAP) + group_ids * CAP + slot_of).astype(jnp.int32)
    pair_count = N_DP * IG * LEN * TOP
    token_count = N_DP * IG * LEN
    pair_of = jnp.full((EXPERTS * N_DP * CAP,), pair_count, jnp.int32)
    pair_of = pair_of.at[target.reshape(-1)].set(jnp.arange(pair_count, dtype=jnp.int32))
    pair_of = pair_of.reshape(EXPERTS, N_DP * CAP)

    def forward(params):
        tokens_f, time_f, class_f, modulation_f, qkv_f, out_f, router_f, up_f, down_f, expert_up_f, expert_down_f = params
        cond = time_f[time_steps] + class_f[class_labels]
        scaled = low(jax.nn.silu(cond))
        shifts = exact_dot(scaled, modulation_f).reshape(ITEMS, 6, 1, D)
        weights = (qkv_f, out_f, router_f, up_f, down_f)
        residual, hidden_mid, logits, shared_out = lax.map(jax.checkpoint(partial(item_block, weights)), (tokens_f, shifts, item_lengths))
        picked = jnp.take_along_axis(logits, routes, axis=-1)
        top_pick = lax.optimization_barrier(jnp.max(picked, axis=-1, keepdims=True))
        exp_terms = jnp.exp(picked - top_pick)
        gates = low(exp_terms / lax.optimization_barrier(jnp.sum(exp_terms, axis=-1, keepdims=True)))
        rows_pad = jnp.concatenate([hidden_mid.reshape(token_count, D), jnp.zeros((1, D), jnp.float32)], axis=0)
        gates_pad = jnp.concatenate([gates.reshape(-1), jnp.zeros((1,), jnp.float32)])

        def expert_step(carry, expert_args):
            up_one, down_one, pair_ids = expert_args
            part_rows = jax.checkpoint(expert_rows)(rows_pad, gates_pad, up_one, down_one, pair_ids)
            return (carry.at[pair_ids // TOP].add(part_rows), None)
        summed, unused = lax.scan(expert_step, jnp.zeros((token_count + 1, D), jnp.float32), (expert_up_f, expert_down_f, pair_of))
        moe = low_back(shared_out + summed[:token_count].reshape(ITEMS, LEN, D))
        return residual + shifts[:, 5] * moe
    floats = tuple((array.astype(jnp.float32) for array in (tokens, time_table, class_table, modulation, qkv_weight, out_weight, router, shared_up, shared_down, expert_up, expert_down)))
    output, pullback = jax.vjp(forward, floats)
    grads = pullback(cotangent.astype(jnp.float32))[0]
    return (output.astype(jnp.bfloat16), grads[0], grads[1], grads[2], grads[3], grads[4], grads[5], grads[6], grads[7], grads[8], grads[9], grads[10])
```

```python
import functools

import jax
import jax.numpy as jnp
from jax import lax
from jax.experimental import pallas as pl
from jax.experimental.pallas import tpu as pltpu
from jax.sharding import PartitionSpec as P

HEADS = 12
HDIM = 64
F32 = jnp.float32
BF16 = jnp.bfloat16
MASKED = -1e30


def layer_norm(values):
    center = values - jnp.mean(values, axis=-1, keepdims=True)
    inverse = lax.rsqrt(jnp.mean(center * center, axis=-1, keepdims=True) + 1e-06)
    return (center * inverse, inverse)


def norm_back(grad_norm, normed, inverse):
    first = jnp.mean(grad_norm, axis=-1, keepdims=True)
    second = jnp.mean(grad_norm * normed, axis=-1, keepdims=True)
    return inverse * (grad_norm - first - normed * second)


def gelu_pair(values):
    square = values * values
    tanh = jnp.tanh(0.7978845608028654 * (values + 0.044715 * values * square))
    half = 0.5 * (1.0 + tanh)
    slope = half + 0.5 * values * (1.0 - tanh * tanh) * (
        0.7978845608028654 * (1.0 + 3.0 * 0.044715 * square)
    )
    return values * half, slope


def silu_back(cond, grad_out):
    return jax.vjp(jax.nn.silu, cond)[1](grad_out)[0]


def exact_dot(left, right):
    return jnp.dot(left, right, precision=lax.Precision.HIGHEST, preferred_element_type=F32)


def dot(left, right):
    return jnp.dot(left, right, preferred_element_type=F32)


def dot_t(left, right):
    return lax.dot_general(left, right, (((1,), (1,)), ((), ())), preferred_element_type=F32)


def t_dot(left, right):
    return lax.dot_general(left, right, (((0,), (0,)), ((), ())), preferred_element_type=F32)


def exchange(values, axis):
    return lax.all_to_all(values, axis, split_axis=0, concat_axis=0, tiled=True)


def copies(values, axis):
    count = lax.axis_size(axis)
    return exchange(jnp.broadcast_to(values[None], (count,) + values.shape), axis)


def small_sum(values, axis):
    return jnp.sum(copies(values, axis), axis=0)


def attend_kernel(length_ref, query_ref, all_ref, out_ref, log_ref, *, heads):
    cols = heads * HDIM
    item = pl.program_id(0)
    queries = query_ref.shape[1]
    full = all_ref.shape[1]
    valid = lax.broadcasted_iota(jnp.int32, (full, queries), 0) < length_ref[item]
    mixed = []
    logs = []
    for head in range(heads):
        at = head * HDIM
        query = query_ref[0, :, at : at + HDIM]
        key = all_ref[0, :, cols + at : cols + at + HDIM]
        value = all_ref[0, :, 2 * cols + at : 2 * cols + at + HDIM]
        scores = jnp.where(valid, dot_t(key, query) * HDIM ** (-0.5), MASKED)
        top = jnp.max(scores, axis=0, keepdims=True)
        terms = jnp.exp(scores - top)
        total = jnp.sum(terms, axis=0, keepdims=True)
        soft = (terms * (1.0 / total)).astype(BF16)
        mixed.append(t_dot(value, soft))
        logs.append(top + jnp.log(total))
    out_ref[0] = jnp.concatenate(mixed, axis=0).T.astype(BF16)
    log_ref[0] = jnp.concatenate(logs + [logs[0]] * (8 - heads), axis=0)


def attend_back_kernel(
    length_ref, query_ref, grad_ref, all_ref, log_ref, out_ref, key_acc, value_acc, *, heads
):
    cols = heads * HDIM
    item = pl.program_id(0)
    step = pl.program_id(1)
    queries = query_ref.shape[1]
    full = all_ref.shape[1]
    valid = lax.broadcasted_iota(jnp.int32, (full, queries), 0) < length_ref[item]

    @pl.when(step == 0)
    def _():
        key_acc[...] = jnp.zeros_like(key_acc)
        value_acc[...] = jnp.zeros_like(value_acc)

    query_grads = []
    for head in range(heads):
        at = head * HDIM
        query = query_ref[0, :, at : at + HDIM]
        grad = grad_ref[0, :, at : at + HDIM]
        key = all_ref[0, :, cols + at : cols + at + HDIM]
        value = all_ref[0, :, 2 * cols + at : 2 * cols + at + HDIM]
        scores = jnp.where(valid, dot_t(key, query) * HDIM ** (-0.5), MASKED)
        soft = jnp.exp(scores - log_ref[0, head : head + 1, :])
        grad_soft = dot_t(value, grad)
        mean = jnp.sum(soft * grad_soft, axis=0, keepdims=True)
        grad_scores = (soft * (grad_soft - mean)).astype(BF16)
        value_acc[head] += dot(soft.astype(BF16), grad)
        key_acc[head] += dot(grad_scores, query)
        query_grads.append(t_dot(key, grad_scores))
    grad_query = jnp.concatenate(query_grads, axis=0).T * HDIM ** (-0.5)
    out_ref[0, pl.ds(pl.multiple_of(step * queries, queries), queries), 0:cols] = grad_query.astype(BF16)

    @pl.when(step == pl.num_programs(1) - 1)
    def _():
        rest = [key_acc[head] * HDIM ** (-0.5) for head in range(heads)]
        rest += [value_acc[head] for head in range(heads)]
        out_ref[0, :, cols:] = jnp.concatenate(rest, axis=1).astype(BF16)


def attend(projected, lengths):
    items, full, three = projected.shape
    cols = three // 3
    heads = cols // HDIM
    queries = min(256, full)
    return pl.pallas_call(
        functools.partial(attend_kernel, heads=heads),
        grid_spec=pltpu.PrefetchScalarGridSpec(
            num_scalar_prefetch=1,
            grid=(items, full // queries),
            in_specs=[
                pl.BlockSpec((1, queries, three), lambda i, q, n: (i, q, 0)),
                pl.BlockSpec((1, full, three), lambda i, q, n: (i, 0, 0)),
            ],
            out_specs=[
                pl.BlockSpec((1, queries, cols), lambda i, q, n: (i, q, 0)),
                pl.BlockSpec((1, 8, queries), lambda i, q, n: (i, 0, q)),
            ],
        ),
        out_shape=[
            jax.ShapeDtypeStruct((items, full, cols), BF16),
            jax.ShapeDtypeStruct((items, 8, full), F32),
        ],
        name="attend",
    )(lengths, projected, projected)


def attend_back(projected, grad_attended, logs, lengths):
    items, full, three = projected.shape
    cols = three // 3
    heads = cols // HDIM
    queries = min(256, full)
    return pl.pallas_call(
        functools.partial(attend_back_kernel, heads=heads),
        grid_spec=pltpu.PrefetchScalarGridSpec(
            num_scalar_prefetch=1,
            grid=(items, full // queries),
            in_specs=[
                pl.BlockSpec((1, queries, three), lambda i, q, n: (i, q, 0)),
                pl.BlockSpec((1, queries, cols), lambda i, q, n: (i, q, 0)),
                pl.BlockSpec((1, full, three), lambda i, q, n: (i, 0, 0)),
                pl.BlockSpec((1, 8, queries), lambda i, q, n: (i, 0, q)),
            ],
            out_specs=pl.BlockSpec((1, full, three), lambda i, q, n: (i, 0, 0)),
            scratch_shapes=[
                pltpu.VMEM((heads, full, HDIM), F32),
                pltpu.VMEM((heads, full, HDIM), F32),
            ],
        ),
        out_shape=jax.ShapeDtypeStruct((items, full, three), BF16),
        name="attend_back",
    )(lengths, projected, grad_attended, projected, logs)


class HeadSplit:
    def __init__(self, tokens, qkv_weight, out_weight, lengths):
        self.hid = lax.axis_size("hid")
        self.items, self.local, self.width = tokens.shape
        self.cols = self.width // self.hid
        self.lengths = lengths
        own = qkv_weight.shape[0]
        parts = qkv_weight.reshape(own, 3, self.hid, self.cols).transpose(2, 0, 1, 3)
        self.qkv = exchange(parts.reshape(self.hid, own, 3 * self.cols), "hid").reshape(
            self.width, 3 * self.cols
        )
        self.out = lax.all_gather(out_weight, "hid", axis=0, tiled=True)
        tokens_all = lax.all_gather(tokens[None], "hid", axis=0, tiled=True)
        self.tokens_all = tokens_all.transpose(1, 0, 2, 3).reshape(
            self.items, self.hid * self.local, self.width
        )

    def to_heads(self, rows):
        parts = rows.reshape(self.items, self.local, self.hid, self.cols).transpose(2, 0, 1, 3)
        return (
            exchange(parts, "hid")
            .transpose(1, 0, 2, 3)
            .reshape(self.items, self.hid * self.local, self.cols)
        )

    def to_rows(self, columns):
        parts = columns.reshape(self.items, self.hid, self.local, self.cols).transpose(1, 0, 2, 3)
        return exchange(parts, "hid").transpose(1, 2, 0, 3).reshape(
            self.items * self.local, self.width
        )

    def forward(self, shift_in, scale_in):
        normed, _ = layer_norm(self.tokens_all.astype(F32))
        hidden = (normed * (1.0 + scale_in) + shift_in).astype(BF16)
        self.hidden = hidden.reshape(-1, self.width)
        self.projected = (
            dot(self.hidden, self.qkv).astype(BF16).reshape(self.items, -1, 3 * self.cols)
        )
        attended, self.logs = attend(self.projected, self.lengths)
        self.attended = self.to_rows(attended)
        return dot(self.attended, self.out)

    def backward(self, grad_branch):
        out_grad = t_dot(self.attended, grad_branch)
        grad_attended = dot_t(grad_branch, self.out).astype(BF16)
        grad_heads = self.to_heads(grad_attended.reshape(self.items, self.local, self.width))
        grad_projected = attend_back(self.projected, grad_heads, self.logs, self.lengths)
        rows = grad_projected.reshape(-1, 3 * self.cols)
        grad_part = dot_t(rows, self.qkv).astype(BF16)
        grad_part = grad_part.reshape(self.items, self.hid, self.local, self.width)
        grad_in = lax.psum_scatter(
            grad_part.transpose(1, 0, 2, 3), "hid", scatter_dimension=0, tiled=True
        )[0].astype(F32)
        qkv_grad = t_dot(self.hidden, rows)
        return grad_in, qkv_grad, out_grad

    def join_qkv(self, parts):
        chunk = parts.shape[1]
        return (
            parts.reshape(self.hid, chunk, 3, self.cols)
            .transpose(1, 2, 0, 3)
            .reshape(chunk, 3 * self.width)
        )


class PatchSplit:
    def __init__(self, tokens, qkv_weight, out_weight, lengths):
        self.hid = lax.axis_size("hid")
        self.items, self.local, self.width = tokens.shape
        self.tokens = tokens
        self.lengths = lengths
        self.qkv = lax.all_gather(qkv_weight, "hid", axis=0, tiled=True)
        self.out = lax.all_gather(out_weight, "hid", axis=0, tiled=True)

    def scores(self):
        positions = jnp.arange(self.hid * self.local, dtype=jnp.int32).reshape(
            self.hid, self.local
        )
        valid = (positions[None] < self.lengths[:, None, None])[:, None, None]
        raw = jnp.einsum("iqhd,kilhd->ihqkl", self.queries, self.keys, preferred_element_type=F32)
        return jnp.where(valid, raw * HDIM ** (-0.5), MASKED)

    def forward(self, shift_in, scale_in):
        items, local, width = self.items, self.local, self.width
        normed, _ = layer_norm(self.tokens.astype(F32))
        hidden = (normed * (1.0 + scale_in) + shift_in).astype(BF16)
        self.hidden = hidden.reshape(-1, width)
        projected = dot(self.hidden, self.qkv).astype(BF16).reshape(items, local, 3 * width)
        self.queries = projected[:, :, :width].reshape(items, local, HEADS, HDIM)
        gathered = lax.all_gather(projected[None, :, :, width:], "hid", axis=0, tiled=True)
        shape = (self.hid, items, local, HEADS, HDIM)
        self.keys = gathered[..., :width].reshape(shape)
        self.values = gathered[..., width:].reshape(shape)
        scores = self.scores()
        top = jnp.max(scores, axis=(3, 4), keepdims=True)
        total = jnp.sum(jnp.exp(scores - top), axis=(3, 4), keepdims=True)
        self.log_total = top + jnp.log(total)
        soft_low = jnp.exp(scores - self.log_total).astype(BF16)
        attended = jnp.einsum("ihqkl,kilhd->iqhd", soft_low, self.values, preferred_element_type=F32)
        self.attended = attended.astype(BF16).reshape(-1, width)
        return dot(self.attended, self.out)

    def backward(self, grad_branch):
        items, local, width = self.items, self.local, self.width
        out_grad = t_dot(self.attended, grad_branch)
        grad_attended = dot_t(grad_branch, self.out).astype(BF16)
        grad_attended = grad_attended.reshape(items, local, HEADS, HDIM)
        soft = jnp.exp(self.scores() - self.log_total)
        grad_soft = jnp.einsum(
            "iqhd,kilhd->ihqkl", grad_attended, self.values, preferred_element_type=F32
        )
        mean = jnp.sum(soft * grad_soft, axis=(3, 4), keepdims=True)
        grad_scores = (soft * (grad_soft - mean)).astype(BF16)
        grad_queries = (
            jnp.einsum("ihqkl,kilhd->iqhd", grad_scores, self.keys, preferred_element_type=F32)
            * HDIM ** (-0.5)
        )
        grad_keys = (
            jnp.einsum("ihqkl,iqhd->kilhd", grad_scores, self.queries, preferred_element_type=F32)
            * HDIM ** (-0.5)
        )
        grad_values = jnp.einsum(
            "ihqkl,iqhd->kilhd", soft.astype(BF16), grad_attended, preferred_element_type=F32
        )
        shape = (self.hid, items, local, width)
        grad_kv = jnp.concatenate([grad_keys.reshape(shape), grad_values.reshape(shape)], axis=-1)
        own = lax.psum_scatter(grad_kv.astype(BF16), "hid", scatter_dimension=0, tiled=True)[0]
        rows = jnp.concatenate(
            [grad_queries.reshape(items, local, width).astype(BF16), own], axis=-1
        ).reshape(-1, 3 * width)
        grad_in = dot_t(rows, self.qkv).reshape(items, local, width)
        return grad_in, t_dot(self.hidden, rows), out_grad

    def join_qkv(self, parts):
        return jnp.sum(parts.astype(F32), axis=0).astype(BF16)


def spread_rows(grad):
    hid, dp = lax.axis_size("hid"), lax.axis_size("dp")
    rows, cols = grad.shape
    parts = grad.astype(BF16).reshape(hid, dp, rows // (hid * dp), cols).transpose(1, 0, 2, 3)
    summed = jnp.sum(exchange(parts, "dp").astype(F32), axis=0).astype(BF16)
    return exchange(summed, "hid")


def dp_sum(grad):
    dp = lax.axis_size("dp")
    rows, cols = grad.shape
    parts = exchange(grad.astype(BF16).reshape(dp, rows // dp, cols), "dp")
    return jnp.sum(parts.astype(F32), axis=0).astype(BF16)


def dp_join(rows):
    return lax.all_gather(rows, "dp", axis=0, tiled=True).astype(F32)


def shards(
    tokens,
    cotangent,
    item_lengths,
    time_steps,
    class_labels,
    routes,
    time_table,
    class_table,
    modulation,
    qkv_weight,
    out_weight,
    router,
    shared_up,
    shared_down,
    expert_up,
    expert_down,
):
    hid_count = lax.axis_size("hid")
    dp_count = lax.axis_size("dp")
    hid_rank = lax.axis_index("hid")
    dp_rank = lax.axis_index("dp")
    item_count, local_len, width = tokens.shape
    full_len = routes.shape[1]
    top_count = routes.shape[2]
    capacity = item_count * full_len * top_count * 5 // (4 * dp_count)
    row_count = item_count * local_len
    group_rows = hid_count * row_count
    slot_rows = dp_count * capacity
    own_width = modulation.shape[0]

    split = HeadSplit if HEADS % hid_count == 0 else PatchSplit
    attention = split(tokens, qkv_weight, out_weight, item_lengths)
    cot_all = lax.all_gather(cotangent[None], "hid", axis=0, tiled=True)

    def owned_rows(table, index):
        rows = table.shape[0]
        local = index - hid_rank * rows
        picked = jnp.take(table, jnp.clip(local, 0, rows - 1), axis=0).astype(F32)
        return jnp.where(((local >= 0) & (local < rows))[:, None], picked, 0.0)

    cond = small_sum(
        owned_rows(time_table, time_steps) + owned_rows(class_table, class_labels), "hid"
    )
    scaled = jax.nn.silu(cond).astype(BF16)
    scaled_own = lax.dynamic_slice_in_dim(scaled, hid_rank * own_width, own_width, 1)
    router_slot = lax.dynamic_update_slice_in_dim(
        jnp.zeros((dp_count, width), F32), router.T.astype(F32), hid_rank * own_width, 1
    )
    early = small_sum(
        jnp.concatenate([dot(scaled_own, modulation), router_slot.reshape(1, -1)], axis=1)
        if item_count == 1
        else jnp.concatenate(
            [dot(scaled_own, modulation).reshape(1, -1), router_slot.reshape(1, -1)], axis=1
        ),
        "hid",
    )
    shift_size = item_count * 6 * width
    shifts = early[:, :shift_size].reshape(item_count, 6, 1, width)
    router_rows = early[:, shift_size:].reshape(dp_count, width).astype(BF16)
    shift_in = shifts[:, 0]
    scale_in = shifts[:, 1]
    gate_in = shifts[:, 2]
    shift_mid = shifts[:, 3]
    scale_mid = shifts[:, 4]
    gate_mid = shifts[:, 5]

    group_routes = (
        routes.reshape(item_count, hid_count, local_len, top_count)
        .transpose(1, 0, 2, 3)
        .reshape(group_rows, top_count)
    )
    pair_routes = group_routes.reshape(-1)
    expert_hot = (pair_routes[:, None] == jnp.arange(dp_count, dtype=jnp.int32)[None, :]).astype(
        jnp.int32
    )
    slot_of = jnp.sum(jnp.cumsum(expert_hot, axis=0) * expert_hot, axis=1) - 1
    target = pair_routes * capacity + slot_of
    pair_count = group_rows * top_count
    pair_of = (
        jnp.full((slot_rows,), pair_count, jnp.int32)
        .at[target]
        .set(jnp.arange(pair_count, dtype=jnp.int32), unique_indices=True, mode="promise_in_bounds")
    )
    token_of = pair_of // top_count
    swapped = jnp.concatenate([group_routes[:, ::-1].reshape(-1), jnp.zeros((1,), jnp.int32)])
    other_out = swapped.at[pair_of].get(mode="promise_in_bounds").reshape(dp_count, 1, capacity)
    other = exchange(other_out, "dp").reshape(slot_rows, 1)
    target_pairs = target.reshape(group_rows, top_count)

    grad_rows = (gate_mid[None] * cot_all.astype(F32)).astype(BF16).reshape(group_rows, width)
    grads_pad = jnp.concatenate([grad_rows, jnp.zeros((8, width), BF16)], axis=0)
    send_grads = grads_pad.at[token_of].get(mode="promise_in_bounds")
    expert_grads = exchange(send_grads.reshape(dp_count, capacity, width), "dp").reshape(
        slot_rows, width
    )

    tokens_f = tokens.astype(F32)
    normed_in, inverse_in = layer_norm(tokens_f)
    branch = attention.forward(shift_in, scale_in).reshape(item_count, local_len, width)
    residual = tokens_f + gate_in * branch
    normed_mid, inverse_mid = layer_norm(residual)
    hidden_mid = (normed_mid * (1.0 + scale_mid) + shift_mid).astype(BF16)
    mid_rows = lax.all_gather(hidden_mid[None], "hid", axis=0, tiled=True).reshape(
        group_rows, width
    )
    send_rows = mid_rows.at[jnp.minimum(token_of, group_rows - 1)].get(mode="promise_in_bounds")
    expert_rows = exchange(send_rows.reshape(dp_count, capacity, width), "dp").reshape(
        slot_rows, width
    )

    shared_gelu, shared_slope = gelu_pair(dot(mid_rows, shared_up))
    shared_act = shared_gelu.astype(BF16)
    grad_shared_pre = (dot_t(grad_rows, shared_down) * shared_slope).astype(BF16)
    grad_mid_part = dot_t(grad_shared_pre, shared_up)
    shared_out = dot(shared_act, shared_down)

    up, down = expert_up[0], expert_down[0]
    logits = dot_t(expert_rows, router_rows)
    ranks = jnp.arange(dp_count, dtype=jnp.int32)[None, :]
    own_hot = (ranks == dp_rank).astype(F32)
    other_hot = (ranks == other).astype(F32)
    gap = jnp.sum(logits * (other_hot - own_hot), axis=1, keepdims=True)
    gate_full = 1.0 / (1.0 + jnp.exp(gap))
    gate_rest = 1.0 / (1.0 + jnp.exp(-gap))
    gate = gate_full.astype(BF16).astype(F32)
    expert_gelu, expert_slope = gelu_pair(dot(expert_rows, up))
    grad_expert_act = dot_t(expert_grads, down)
    grad_gate = jnp.sum(grad_expert_act * expert_gelu, axis=1, keepdims=True)
    grad_expert_pre = (grad_expert_act * gate * expert_slope).astype(BF16)
    grad_logits = (gate_full * gate_rest * grad_gate) * (own_hot - other_hot)
    logits_high = grad_logits.astype(BF16)
    logits_low = (grad_logits - logits_high.astype(F32)).astype(BF16)
    slot_grads = (
        dot_t(grad_expert_pre, up) + dot(logits_high, router_rows) + dot(logits_low, router_rows)
    ).astype(BF16)
    back_rows = exchange(slot_grads.reshape(dp_count, capacity, width), "dp").reshape(
        slot_rows, width
    )
    expert_act = (gate * expert_gelu).astype(BF16)
    expert_out = dot(expert_act, down).astype(BF16)
    returned = exchange(expert_out.reshape(dp_count, capacity, width), "dp").reshape(
        slot_rows, width
    )
    router_part = t_dot(logits_high, expert_rows) + t_dot(logits_low, expert_rows)
    expert_down_grad = t_dot(expert_act, expert_grads)[None]
    expert_up_grad = t_dot(expert_rows, grad_expert_pre)[None]
    shared_down_rows = dp_sum(t_dot(shared_act, grad_rows))
    shared_up_rows = dp_sum(t_dot(mid_rows, grad_shared_pre))

    def combine(rows, start):
        total = start
        for j in range(top_count):
            total = total + rows.at[target_pairs[:, j]].get(mode="promise_in_bounds").astype(F32)
        return lax.psum_scatter(
            total.astype(BF16).reshape(hid_count, item_count, local_len, width),
            "hid",
            scatter_dimension=0,
            tiled=True,
        )[0].astype(F32)

    grad_mid = combine(back_rows, grad_mid_part)
    grad_out = cotangent.astype(F32)
    grad_scale_mid = jnp.sum(grad_mid * normed_mid, axis=1)
    grad_shift_mid = jnp.sum(grad_mid, axis=1)
    grad_residual = grad_out + norm_back(grad_mid * (1.0 + scale_mid), normed_mid, inverse_mid)
    grad_gate_in = jnp.sum(grad_residual * branch, axis=1)
    grad_branch = (gate_in * grad_residual).astype(BF16).reshape(row_count, width)

    moe = combine(returned, shared_out)
    output = (residual + gate_mid * moe).astype(BF16)
    grad_gate_mid = jnp.sum(grad_out * moe, axis=1)

    grad_in, qkv_grad, out_grad = attention.backward(grad_branch)
    grad_scale_in = jnp.sum(grad_in * normed_in, axis=1)
    grad_shift_in = jnp.sum(grad_in, axis=1)
    tokens_grad = grad_residual + norm_back(grad_in * (1.0 + scale_in), normed_in, inverse_in)

    grad_shifts = jnp.stack(
        [grad_shift_in, grad_scale_in, grad_gate_in, grad_shift_mid, grad_scale_mid, grad_gate_mid],
        axis=1,
    ).reshape(item_count, 6 * width)
    shifts_all = lax.all_gather(small_sum(grad_shifts, "hid"), "dp", axis=0, tiled=True)
    marks = jnp.stack([time_steps, class_labels], axis=1).astype(F32)
    notes = lax.all_gather(jnp.concatenate([cond, marks], axis=1), "dp", axis=0, tiled=True)
    cond_own = lax.dynamic_slice_in_dim(notes[:, :width], hid_rank * own_width, own_width, 1)
    scaled_all = jax.nn.silu(cond_own).astype(BF16).astype(F32)
    modulation_grad = exact_dot(scaled_all.T, shifts_all)
    grad_cond_own = silu_back(cond_own, exact_dot(shifts_all, modulation.astype(F32).T))
    grad_cond = copies(grad_cond_own, "hid").transpose(1, 0, 2).reshape(-1, width)

    def table_grad(table, index):
        rows = table.shape[0]
        positions = (hid_rank * rows + jnp.arange(rows, dtype=jnp.int32)).astype(F32)
        return exact_dot((positions[:, None] == index[None, :]).astype(F32), grad_cond)

    time_grad = table_grad(time_table, notes[:, width])
    class_grad = table_grad(class_table, notes[:, width + 1])

    router_sum = small_sum(small_sum(router_part, "hid"), "dp")
    router_grad = lax.dynamic_slice_in_dim(router_sum, hid_rank * own_width, own_width, 1).T

    out_rows = jnp.sum(spread_rows(out_grad).astype(F32), axis=0).astype(BF16)
    qkv_rows = attention.join_qkv(spread_rows(qkv_grad))
    return (
        output,
        tokens_grad,
        time_grad,
        class_grad,
        modulation_grad,
        dp_join(qkv_rows),
        dp_join(out_rows),
        router_grad,
        dp_join(shared_up_rows),
        dp_join(shared_down_rows),
        expert_up_grad,
        expert_down_grad,
    )


def solution(mesh):
    placed = (
        P("dp", "hid", None),
        P("dp", "hid", None),
        P("dp"),
        P("dp"),
        P("dp"),
        P("dp", None, None),
        P("hid", None),
        P("hid", None),
        P("hid", None),
        P("hid", None),
        P("hid", None),
        P("hid", None),
        P(None, "hid"),
        P("hid", None),
        P("dp", None, "hid"),
        P("dp", "hid", None),
    )
    return jax.shard_map(
        shards,
        mesh=mesh,
        in_specs=placed,
        out_specs=(
            P("dp", "hid", None),
            P("dp", "hid", None),
            P("hid", None),
            P("hid", None),
            P("hid", None),
            P("hid", None),
            P("hid", None),
            P("hid", None),
            P(None, "hid"),
            P("hid", None),
            P("dp", None, "hid"),
            P("dp", "hid", None),
        ),
        check_vma=False,
    )
```

```python
import functools

import jax
import jax.numpy as jnp
from jax import lax
from jax.experimental import pallas as pl
from jax.experimental.pallas import tpu as pltpu
from jax.sharding import PartitionSpec as P

HEADS = 12
HDIM = 64
F32 = jnp.float32
BF16 = jnp.bfloat16
MASKED = -1e30


def layer_norm(values):
    center = values - jnp.mean(values, axis=-1, keepdims=True)
    inverse = lax.rsqrt(jnp.mean(center * center, axis=-1, keepdims=True) + 1e-06)
    return (center * inverse, inverse)


def norm_back(grad_norm, normed, inverse):
    first = jnp.mean(grad_norm, axis=-1, keepdims=True)
    second = jnp.mean(grad_norm * normed, axis=-1, keepdims=True)
    return inverse * (grad_norm - first - normed * second)


def gelu_pair(values):
    square = values * values
    tanh = jnp.tanh(0.7978845608028654 * (values + 0.044715 * values * square))
    half = 0.5 * (1.0 + tanh)
    slope = half + 0.5 * values * (1.0 - tanh * tanh) * (
        0.7978845608028654 * (1.0 + 3.0 * 0.044715 * square)
    )
    return values * half, slope


def tie(*values):
    return lax.optimization_barrier(values)


def silu_back(cond, grad_out):
    return jax.vjp(jax.nn.silu, cond)[1](grad_out)[0]


def exact_dot(left, right):
    return jnp.dot(left, right, precision=lax.Precision.HIGHEST, preferred_element_type=F32)


def dot(left, right):
    return jnp.dot(left, right, preferred_element_type=F32)


def dot_t(left, right):
    return lax.dot_general(left, right, (((1,), (1,)), ((), ())), preferred_element_type=F32)


def t_dot(left, right):
    return lax.dot_general(left, right, (((0,), (0,)), ((), ())), preferred_element_type=F32)


def exchange(values, axis):
    return lax.all_to_all(values, axis, split_axis=0, concat_axis=0, tiled=True)


def copies(values, axis):
    count = lax.axis_size(axis)
    return exchange(jnp.broadcast_to(values[None], (count,) + values.shape), axis)


def small_sum(values, axis):
    return jnp.sum(copies(values, axis), axis=0)


def attend_kernel(length_ref, query_ref, all_ref, out_ref, log_ref, *, heads):
    cols = heads * HDIM
    item = pl.program_id(0)
    queries = query_ref.shape[1]
    full = all_ref.shape[1]
    valid = lax.broadcasted_iota(jnp.int32, (full, queries), 0) < length_ref[item]
    mixed = []
    logs = []
    for head in range(heads):
        at = head * HDIM
        query = query_ref[0, :, at : at + HDIM]
        key = all_ref[0, :, cols + at : cols + at + HDIM]
        value = all_ref[0, :, 2 * cols + at : 2 * cols + at + HDIM]
        scores = jnp.where(valid, dot_t(key, query) * HDIM ** (-0.5), MASKED)
        top = jnp.max(scores, axis=0, keepdims=True)
        terms = jnp.exp(scores - top)
        total = jnp.sum(terms, axis=0, keepdims=True)
        soft = (terms * (1.0 / total)).astype(BF16)
        mixed.append(t_dot(value, soft))
        logs.append(top + jnp.log(total))
    out_ref[0] = jnp.concatenate(mixed, axis=0).T.astype(BF16)
    log_ref[0] = jnp.concatenate(logs + [logs[0]] * (8 - heads), axis=0)


def attend_back_kernel(
    length_ref, query_ref, grad_ref, all_ref, log_ref, out_ref, key_acc, value_acc, *, heads
):
    cols = heads * HDIM
    item = pl.program_id(0)
    step = pl.program_id(1)
    queries = query_ref.shape[1]
    full = all_ref.shape[1]
    valid = lax.broadcasted_iota(jnp.int32, (full, queries), 0) < length_ref[item]

    @pl.when(step == 0)
    def _():
        key_acc[...] = jnp.zeros_like(key_acc)
        value_acc[...] = jnp.zeros_like(value_acc)

    query_grads = []
    for head in range(heads):
        at = head * HDIM
        query = query_ref[0, :, at : at + HDIM]
        grad = grad_ref[0, :, at : at + HDIM]
        key = all_ref[0, :, cols + at : cols + at + HDIM]
        value = all_ref[0, :, 2 * cols + at : 2 * cols + at + HDIM]
        scores = jnp.where(valid, dot_t(key, query) * HDIM ** (-0.5), MASKED)
        soft = jnp.exp(scores - log_ref[0, head : head + 1, :])
        grad_soft = dot_t(value, grad)
        mean = jnp.sum(soft * grad_soft, axis=0, keepdims=True)
        grad_scores = (soft * (grad_soft - mean)).astype(BF16)
        value_acc[head] += dot(soft.astype(BF16), grad)
        key_acc[head] += dot(grad_scores, query)
        query_grads.append(t_dot(key, grad_scores))
    grad_query = jnp.concatenate(query_grads, axis=0).T * HDIM ** (-0.5)
    out_ref[0, pl.ds(pl.multiple_of(step * queries, queries), queries), 0:cols] = grad_query.astype(BF16)

    @pl.when(step == pl.num_programs(1) - 1)
    def _():
        rest = [key_acc[head] * HDIM ** (-0.5) for head in range(heads)]
        rest += [value_acc[head] for head in range(heads)]
        out_ref[0, :, cols:] = jnp.concatenate(rest, axis=1).astype(BF16)


def attend(projected, lengths):
    items, full, three = projected.shape
    cols = three // 3
    heads = cols // HDIM
    queries = min(256, full)
    return pl.pallas_call(
        functools.partial(attend_kernel, heads=heads),
        grid_spec=pltpu.PrefetchScalarGridSpec(
            num_scalar_prefetch=1,
            grid=(items, full // queries),
            in_specs=[
                pl.BlockSpec((1, queries, three), lambda i, q, n: (i, q, 0)),
                pl.BlockSpec((1, full, three), lambda i, q, n: (i, 0, 0)),
            ],
            out_specs=[
                pl.BlockSpec((1, queries, cols), lambda i, q, n: (i, q, 0)),
                pl.BlockSpec((1, 8, queries), lambda i, q, n: (i, 0, q)),
            ],
        ),
        out_shape=[
            jax.ShapeDtypeStruct((items, full, cols), BF16),
            jax.ShapeDtypeStruct((items, 8, full), F32),
        ],
        name="attend",
    )(lengths, projected, projected)


def attend_back(projected, grad_attended, logs, lengths):
    items, full, three = projected.shape
    cols = three // 3
    heads = cols // HDIM
    queries = min(256, full)
    return pl.pallas_call(
        functools.partial(attend_back_kernel, heads=heads),
        grid_spec=pltpu.PrefetchScalarGridSpec(
            num_scalar_prefetch=1,
            grid=(items, full // queries),
            in_specs=[
                pl.BlockSpec((1, queries, three), lambda i, q, n: (i, q, 0)),
                pl.BlockSpec((1, queries, cols), lambda i, q, n: (i, q, 0)),
                pl.BlockSpec((1, full, three), lambda i, q, n: (i, 0, 0)),
                pl.BlockSpec((1, 8, queries), lambda i, q, n: (i, 0, q)),
            ],
            out_specs=pl.BlockSpec((1, full, three), lambda i, q, n: (i, 0, 0)),
            scratch_shapes=[
                pltpu.VMEM((heads, full, HDIM), F32),
                pltpu.VMEM((heads, full, HDIM), F32),
            ],
        ),
        out_shape=jax.ShapeDtypeStruct((items, full, three), BF16),
        name="attend_back",
    )(lengths, projected, grad_attended, projected, logs)


def block_of(rows):
    return 256 if rows % 256 == 0 else rows


def dispatch_kernel(target_ref, table_ref, out_ref):
    block = out_ref.shape[0]
    slots = pl.program_id(0) * block + lax.broadcasted_iota(
        jnp.int32, (block, table_ref.shape[0]), 0
    )
    hot = slots == target_ref[0:1, :]
    for j in range(1, target_ref.shape[0]):
        hot = hot | (slots == target_ref[j : j + 1, :])
    out_ref[...] = dot(jnp.where(hot, 1.0, 0.0).astype(BF16), table_ref[...]).astype(BF16)


def dispatch(target_rows, table, slot_rows):
    rows, width = table.shape
    block = block_of(slot_rows)
    return pl.pallas_call(
        dispatch_kernel,
        grid=(slot_rows // block,),
        in_specs=[
            pl.BlockSpec(target_rows.shape, lambda i: (0, 0)),
            pl.BlockSpec((rows, width), lambda i: (0, 0)),
        ],
        out_specs=pl.BlockSpec((block, width), lambda i: (i, 0)),
        out_shape=jax.ShapeDtypeStruct((slot_rows, width), BF16),
        name="dispatch",
    )(target_rows, table)


def combine_kernel(target_ref, rows_ref, start_ref, out_ref):
    slots = lax.broadcasted_iota(jnp.int32, (out_ref.shape[0], rows_ref.shape[0]), 1)
    hot = slots == target_ref[:, 0:1]
    for j in range(1, target_ref.shape[1]):
        hot = hot | (slots == target_ref[:, j : j + 1])
    picked = dot(jnp.where(hot, 1.0, 0.0).astype(BF16), rows_ref[...])
    out_ref[...] = (picked + start_ref[...]).astype(BF16)


def combine(target_pairs, rows, start):
    patches, width = start.shape
    block = block_of(patches)
    return pl.pallas_call(
        combine_kernel,
        grid=(patches // block,),
        in_specs=[
            pl.BlockSpec((block, target_pairs.shape[1]), lambda i: (i, 0)),
            pl.BlockSpec(rows.shape, lambda i: (0, 0)),
            pl.BlockSpec((block, width), lambda i: (i, 0)),
        ],
        out_specs=pl.BlockSpec((block, width), lambda i: (i, 0)),
        out_shape=jax.ShapeDtypeStruct((patches, width), BF16),
        name="combine",
    )(target_pairs, rows, start)


def out_columns(attended, grad_branch, router_part):
    columns = jnp.pad(router_part, ((0, -router_part.shape[0] % 128), (0, 0)))
    return jnp.concatenate([t_dot(attended, grad_branch), columns.T], axis=1)


class HeadSplit:
    def __init__(self, tokens, qkv_weight, out_weight, lengths):
        self.hid = lax.axis_size("hid")
        self.items, self.local, self.width = tokens.shape
        self.cols = self.width // self.hid
        self.lengths = lengths
        dp, rank = lax.axis_size("dp"), lax.axis_index("dp")
        chunk = qkv_weight.shape[0] // dp
        rows = lax.dynamic_slice_in_dim(qkv_weight, rank * chunk, chunk, 0)
        parts = rows.reshape(chunk, 3, self.hid, self.cols).transpose(2, 0, 1, 3)
        parts = exchange(parts.reshape(self.hid, chunk, 3 * self.cols), "hid")
        self.qkv = self.in_order(lax.all_gather(parts, "dp"))
        rows = lax.dynamic_slice_in_dim(out_weight, rank * chunk, chunk, 0)
        self.out = self.in_order(copies(copies(rows, "hid"), "dp"))
        tokens_all = lax.all_gather(tokens[None], "hid", axis=0, tiled=True)
        self.tokens_all = tokens_all.transpose(1, 0, 2, 3).reshape(
            self.items, self.hid * self.local, self.width
        )

    def in_order(self, parts):
        return parts.transpose(1, 0, 2, 3).reshape(self.width, parts.shape[-1])

    def to_heads(self, rows):
        parts = rows.reshape(self.items, self.local, self.hid, self.cols).transpose(2, 0, 1, 3)
        return (
            exchange(parts, "hid")
            .transpose(1, 0, 2, 3)
            .reshape(self.items, self.hid * self.local, self.cols)
        )

    def to_rows(self, columns):
        parts = columns.reshape(self.items, self.hid, self.local, self.cols).transpose(1, 0, 2, 3)
        return exchange(parts, "hid").transpose(1, 2, 0, 3).reshape(
            self.items * self.local, self.width
        )

    def forward(self, shift_in, scale_in):
        normed, _ = layer_norm(self.tokens_all.astype(F32))
        hidden = (normed * (1.0 + scale_in) + shift_in).astype(BF16)
        self.hidden = hidden.reshape(-1, self.width)
        self.projected = (
            dot(self.hidden, self.qkv).astype(BF16).reshape(self.items, -1, 3 * self.cols)
        )
        attended, self.logs = attend(self.projected, self.lengths)
        self.attended = self.to_rows(attended)
        return dot(self.attended, self.out)

    def backward(self, grad_branch, router_part):
        grad_attended = dot_t(grad_branch, self.out).astype(BF16)
        grad_heads = self.to_heads(grad_attended.reshape(self.items, self.local, self.width))
        branch_late, grad_heads = tie(grad_branch, grad_heads)
        out_parts = spread_rows(out_columns(self.attended, branch_late, router_part))
        grad_projected = attend_back(self.projected, grad_heads, self.logs, self.lengths)
        grad_projected, out_parts = tie(grad_projected, out_parts)
        rows = grad_projected.reshape(-1, 3 * self.cols)
        grad_part = dot_t(rows, self.qkv).astype(BF16)
        grad_part = grad_part.reshape(self.items, self.hid, self.local, self.width)
        grad_in = lax.psum_scatter(
            grad_part.transpose(1, 0, 2, 3), "hid", scatter_dimension=0, tiled=True
        )[0].astype(F32)
        qkv_parts = spread_rows(t_dot(self.hidden, rows))
        return grad_in, qkv_parts, out_parts

    def join_qkv(self, parts):
        chunk = parts.shape[1]
        return (
            parts.reshape(self.hid, chunk, 3, self.cols)
            .transpose(1, 2, 0, 3)
            .reshape(chunk, 3 * self.width)
        )


class PatchSplit:
    def __init__(self, tokens, qkv_weight, out_weight, lengths):
        self.hid = lax.axis_size("hid")
        self.items, self.local, self.width = tokens.shape
        self.tokens_all = tokens
        self.lengths = lengths
        self.qkv = lax.all_gather(qkv_weight, "hid", axis=0, tiled=True)
        self.out = lax.all_gather(out_weight, "hid", axis=0, tiled=True)

    def scores(self):
        positions = jnp.arange(self.hid * self.local, dtype=jnp.int32).reshape(
            self.hid, self.local
        )
        valid = (positions[None] < self.lengths[:, None, None])[:, None, None]
        raw = jnp.einsum("iqhd,kilhd->ihqkl", self.queries, self.keys, preferred_element_type=F32)
        return jnp.where(valid, raw * HDIM ** (-0.5), MASKED)

    def forward(self, shift_in, scale_in):
        items, local, width = self.items, self.local, self.width
        normed, _ = layer_norm(self.tokens_all.astype(F32))
        hidden = (normed * (1.0 + scale_in) + shift_in).astype(BF16)
        self.hidden = hidden.reshape(-1, width)
        projected = dot(self.hidden, self.qkv).astype(BF16).reshape(items, local, 3 * width)
        self.queries = projected[:, :, :width].reshape(items, local, HEADS, HDIM)
        gathered = lax.all_gather(projected[None, :, :, width:], "hid", axis=0, tiled=True)
        shape = (self.hid, items, local, HEADS, HDIM)
        self.keys = gathered[..., :width].reshape(shape)
        self.values = gathered[..., width:].reshape(shape)
        scores = self.scores()
        top = jnp.max(scores, axis=(3, 4), keepdims=True)
        total = jnp.sum(jnp.exp(scores - top), axis=(3, 4), keepdims=True)
        self.log_total = top + jnp.log(total)
        soft_low = jnp.exp(scores - self.log_total).astype(BF16)
        attended = jnp.einsum("ihqkl,kilhd->iqhd", soft_low, self.values, preferred_element_type=F32)
        self.attended = attended.astype(BF16).reshape(-1, width)
        return dot(self.attended, self.out)

    def backward(self, grad_branch, router_part):
        items, local, width = self.items, self.local, self.width
        out_parts = spread_rows(out_columns(self.attended, grad_branch, router_part))
        grad_attended = dot_t(grad_branch, self.out).astype(BF16)
        grad_attended = grad_attended.reshape(items, local, HEADS, HDIM)
        soft = jnp.exp(self.scores() - self.log_total)
        grad_soft = jnp.einsum(
            "iqhd,kilhd->ihqkl", grad_attended, self.values, preferred_element_type=F32
        )
        mean = jnp.sum(soft * grad_soft, axis=(3, 4), keepdims=True)
        grad_scores = (soft * (grad_soft - mean)).astype(BF16)
        grad_queries = (
            jnp.einsum("ihqkl,kilhd->iqhd", grad_scores, self.keys, preferred_element_type=F32)
            * HDIM ** (-0.5)
        )
        grad_keys = (
            jnp.einsum("ihqkl,iqhd->kilhd", grad_scores, self.queries, preferred_element_type=F32)
            * HDIM ** (-0.5)
        )
        grad_values = jnp.einsum(
            "ihqkl,iqhd->kilhd", soft.astype(BF16), grad_attended, preferred_element_type=F32
        )
        shape = (self.hid, items, local, width)
        grad_kv = jnp.concatenate([grad_keys.reshape(shape), grad_values.reshape(shape)], axis=-1)
        own = lax.psum_scatter(grad_kv.astype(BF16), "hid", scatter_dimension=0, tiled=True)[0]
        rows = jnp.concatenate(
            [grad_queries.reshape(items, local, width).astype(BF16), own], axis=-1
        ).reshape(-1, 3 * width)
        grad_in = dot_t(rows, self.qkv).reshape(items, local, width)
        return grad_in, spread_rows(t_dot(self.hidden, rows)), out_parts

    def join_qkv(self, parts):
        return jnp.sum(parts.astype(F32), axis=0).astype(BF16)


def spread_rows(grad):
    hid, dp = lax.axis_size("hid"), lax.axis_size("dp")
    rows, cols = grad.shape
    parts = grad.astype(BF16).reshape(hid, dp, rows // (hid * dp), cols).transpose(1, 0, 2, 3)
    return jnp.sum(exchange(parts, "dp").astype(F32), axis=0).astype(BF16)


def dp_parts(grad):
    dp = lax.axis_size("dp")
    rows, cols = grad.shape
    return grad.astype(BF16).reshape(dp, rows // dp, cols)


def dp_sum(parts):
    return jnp.sum(exchange(parts, "dp").astype(F32), axis=0).astype(BF16)


def dp_sums(parts):
    if len({each.shape[2] for each in parts}) > 1:
        return [dp_sum(each) for each in parts]
    summed = dp_sum(jnp.concatenate(parts, axis=1))
    sizes = [each.shape[1] for each in parts]
    return [summed[sum(sizes[:n]) : sum(sizes[: n + 1])] for n in range(len(sizes))]


def dp_join(rows):
    return lax.all_gather(rows, "dp", axis=0, tiled=True).astype(F32)


def shards(
    tokens,
    cotangent,
    item_lengths,
    time_steps,
    class_labels,
    routes,
    time_table,
    class_table,
    modulation,
    qkv_weight,
    out_weight,
    router,
    shared_up,
    shared_down,
    expert_up,
    expert_down,
):
    hid_count = lax.axis_size("hid")
    dp_count = lax.axis_size("dp")
    hid_rank = lax.axis_index("hid")
    dp_rank = lax.axis_index("dp")
    item_count, local_len, width = tokens.shape
    full_len = routes.shape[1]
    top_count = routes.shape[2]
    capacity = item_count * full_len * top_count * 5 // (4 * dp_count)
    row_count = item_count * local_len
    group_rows = hid_count * row_count
    slot_rows = dp_count * capacity
    own_width = modulation.shape[0]

    split = HeadSplit if HEADS % hid_count == 0 else PatchSplit
    attention = split(tokens, qkv_weight, out_weight, item_lengths)
    cot_late, attention.tokens_all = tie(cotangent, attention.tokens_all)
    cot_all = lax.all_gather(cot_late[None], "hid", axis=0, tiled=True)

    def owned_rows(table, index):
        rows = table.shape[0]
        local = index - hid_rank * rows
        picked = jnp.take(table, jnp.clip(local, 0, rows - 1), axis=0).astype(F32)
        return jnp.where(((local >= 0) & (local < rows))[:, None], picked, 0.0)

    cond = small_sum(
        owned_rows(time_table, time_steps) + owned_rows(class_table, class_labels), "hid"
    )
    scaled = jax.nn.silu(cond).astype(BF16)
    scaled_own = lax.dynamic_slice_in_dim(scaled, hid_rank * own_width, own_width, 1)
    router_slot = lax.dynamic_update_slice_in_dim(
        jnp.zeros((dp_count, width), F32), router.T.astype(F32), hid_rank * own_width, 1
    )
    early = small_sum(
        jnp.concatenate([dot(scaled_own, modulation), router_slot.reshape(1, -1)], axis=1)
        if item_count == 1
        else jnp.concatenate(
            [dot(scaled_own, modulation).reshape(1, -1), router_slot.reshape(1, -1)], axis=1
        ),
        "hid",
    )
    shift_size = item_count * 6 * width
    shifts = early[:, :shift_size].reshape(item_count, 6, 1, width)
    router_rows = early[:, shift_size:].reshape(dp_count, width).astype(BF16)
    shift_in = shifts[:, 0]
    scale_in = shifts[:, 1]
    gate_in = shifts[:, 2]
    shift_mid = shifts[:, 3]
    scale_mid = shifts[:, 4]
    gate_mid = shifts[:, 5]

    group_routes = (
        routes.reshape(item_count, hid_count, local_len, top_count)
        .transpose(1, 0, 2, 3)
        .reshape(group_rows, top_count)
    )
    pair_routes = group_routes.reshape(-1)
    expert_hot = (pair_routes[:, None] == jnp.arange(dp_count, dtype=jnp.int32)[None, :]).astype(
        jnp.int32
    )
    slot_of = jnp.sum(jnp.cumsum(expert_hot, axis=0) * expert_hot, axis=1) - 1
    target = pair_routes * capacity + slot_of
    target_pairs = target.reshape(group_rows, top_count)
    target_rows = target_pairs.T
    swapped = group_routes[:, ::-1].reshape(-1)
    slots = jnp.arange(slot_rows, dtype=jnp.int32)
    other_out = jnp.sum(jnp.where(target[:, None] == slots[None, :], swapped[:, None], 0), axis=0)
    other = exchange(other_out.reshape(dp_count, 1, capacity), "dp").reshape(slot_rows, 1)

    marks = jnp.stack([time_steps, class_labels], axis=1).astype(F32)
    notes = lax.all_gather(jnp.concatenate([cond, marks], axis=1), "dp", axis=0, tiled=True)
    attention.tokens_all, notes, other = tie(attention.tokens_all, notes, other)

    grad_rows = (gate_mid[None] * cot_all.astype(F32)).astype(BF16).reshape(group_rows, width)
    send_grads = dispatch(target_rows, grad_rows, slot_rows)

    def to_slots(rows):
        return exchange(rows.reshape(dp_count, capacity, width), "dp").reshape(slot_rows, width)

    tokens_f = tokens.astype(F32)
    normed_in, inverse_in = layer_norm(tokens_f)
    branch = attention.forward(shift_in, scale_in).reshape(item_count, local_len, width)
    residual = tokens_f + gate_in * branch
    normed_mid, inverse_mid = layer_norm(residual)
    hidden_mid = (normed_mid * (1.0 + scale_mid) + shift_mid).astype(BF16)
    hidden_mid, send_grads = tie(hidden_mid, send_grads)
    expert_grads = to_slots(send_grads)
    mid_rows = lax.all_gather(hidden_mid[None], "hid", axis=0, tiled=True).reshape(
        group_rows, width
    )
    send_rows, expert_grads = tie(dispatch(target_rows, mid_rows, slot_rows), expert_grads)
    expert_rows = to_slots(send_rows)

    shared_gelu, shared_slope = gelu_pair(dot(mid_rows, shared_up))
    shared_act = shared_gelu.astype(BF16)
    grad_shared_pre = (dot_t(grad_rows, shared_down) * shared_slope).astype(BF16)
    grad_mid_part = dot_t(grad_shared_pre, shared_up)
    shared_out = dot(shared_act, shared_down)
    down_parts = dp_parts(t_dot(shared_act, grad_rows))
    up_parts = dp_parts(t_dot(mid_rows, grad_shared_pre))
    expert_rows, down_parts, up_parts, grad_mid_part, shared_out = tie(
        expert_rows, down_parts, up_parts, grad_mid_part, shared_out
    )
    shared_down_rows, shared_up_rows = dp_sums([down_parts, up_parts])

    up, down = expert_up[0], expert_down[0]
    logits = dot_t(expert_rows, router_rows)
    ranks = jnp.arange(dp_count, dtype=jnp.int32)[None, :]
    own_hot = (ranks == dp_rank).astype(F32)
    other_hot = (ranks == other).astype(F32)
    gap = jnp.sum(logits * (other_hot - own_hot), axis=1, keepdims=True)
    gate_full = 1.0 / (1.0 + jnp.exp(gap))
    gate_rest = 1.0 / (1.0 + jnp.exp(-gap))
    gate = gate_full.astype(BF16).astype(F32)
    expert_gelu, expert_slope = gelu_pair(dot(expert_rows, up))
    grad_expert_act = dot_t(expert_grads, down)
    grad_gate = jnp.sum(grad_expert_act * expert_gelu, axis=1, keepdims=True)
    grad_expert_pre = (grad_expert_act * gate * expert_slope).astype(BF16)
    grad_logits = (gate_full * gate_rest * grad_gate) * (own_hot - other_hot)
    logits_high = grad_logits.astype(BF16)
    logits_low = (grad_logits - logits_high.astype(F32)).astype(BF16)
    slot_grads = (
        dot_t(grad_expert_pre, up) + dot(logits_high, router_rows) + dot(logits_low, router_rows)
    ).astype(BF16)
    slot_grads, shared_down_rows, shared_up_rows = tie(
        slot_grads, shared_down_rows, shared_up_rows
    )
    back_rows = to_slots(slot_grads)
    expert_act = (gate * expert_gelu).astype(BF16)
    expert_out = dot(expert_act, down).astype(BF16)
    expert_down_grad = t_dot(expert_act, expert_grads)[None]
    expert_up_grad = t_dot(expert_rows, grad_expert_pre)[None]
    router_part = t_dot(logits_high, expert_rows) + t_dot(logits_low, expert_rows)
    back_rows, expert_out, expert_down_grad, expert_up_grad, router_part = tie(
        back_rows, expert_out, expert_down_grad, expert_up_grad, router_part
    )
    returned = to_slots(expert_out)

    def own_patches(rows):
        return lax.psum_scatter(
            rows.reshape(hid_count, item_count, local_len, width),
            "hid",
            scatter_dimension=0,
            tiled=True,
        )[0].astype(F32)

    grad_mid = own_patches(combine(target_pairs, back_rows, grad_mid_part))
    grad_out = cotangent.astype(F32)
    grad_scale_mid = jnp.sum(grad_mid * normed_mid, axis=1)
    grad_shift_mid = jnp.sum(grad_mid, axis=1)
    grad_residual = grad_out + norm_back(grad_mid * (1.0 + scale_mid), normed_mid, inverse_mid)
    grad_gate_in = jnp.sum(grad_residual * branch, axis=1)
    grad_branch = (gate_in * grad_residual).astype(BF16).reshape(row_count, width)

    returned, _ = tie(returned, grad_branch)
    moe = own_patches(combine(target_pairs, returned, shared_out))
    output = (residual + gate_mid * moe).astype(BF16)
    grad_gate_mid = jnp.sum(grad_out * moe, axis=1)

    grad_in, qkv_parts, out_parts = attention.backward(grad_branch, router_part)
    grad_scale_in = jnp.sum(grad_in * normed_in, axis=1)
    grad_shift_in = jnp.sum(grad_in, axis=1)
    tokens_grad = grad_residual + norm_back(grad_in * (1.0 + scale_in), normed_in, inverse_in)

    grad_shifts = jnp.stack(
        [grad_shift_in, grad_scale_in, grad_gate_in, grad_shift_mid, grad_scale_mid, grad_gate_mid],
        axis=1,
    ).reshape(item_count, 6 * width)
    shifts_all = lax.all_gather(small_sum(grad_shifts, "hid"), "dp", axis=0, tiled=True)
    cond_own = lax.dynamic_slice_in_dim(notes[:, :width], hid_rank * own_width, own_width, 1)
    scaled_all = jax.nn.silu(cond_own).astype(BF16).astype(F32)
    modulation_grad = exact_dot(scaled_all.T, shifts_all)
    grad_cond_own = silu_back(cond_own, exact_dot(shifts_all, modulation.astype(F32).T))
    grad_cond = copies(grad_cond_own, "hid").transpose(1, 0, 2).reshape(-1, width)

    def table_grad(table, index):
        rows = table.shape[0]
        positions = (hid_rank * rows + jnp.arange(rows, dtype=jnp.int32)).astype(F32)
        return exact_dot((positions[:, None] == index[None, :]).astype(F32), grad_cond)

    time_grad = table_grad(time_table, notes[:, width])
    class_grad = table_grad(class_table, notes[:, width + 1])

    blocks = exchange(jnp.concatenate([qkv_parts, out_parts], axis=2), "hid")
    qkv_cols = qkv_parts.shape[2]
    out_rows = jnp.sum(blocks[:, :, qkv_cols:].astype(F32), axis=0).astype(BF16)
    qkv_rows = attention.join_qkv(blocks[:, :, :qkv_cols])
    joined = dp_join(jnp.concatenate([qkv_rows, out_rows], axis=1))
    qkv_size = 3 * width
    return (
        output,
        tokens_grad,
        time_grad,
        class_grad,
        modulation_grad,
        joined[:, :qkv_size],
        joined[:, qkv_size : qkv_size + width],
        joined[:, qkv_size + width : qkv_size + width + dp_count],
        dp_join(shared_up_rows),
        dp_join(shared_down_rows),
        expert_up_grad,
        expert_down_grad,
    )


def solution(mesh):
    placed = (
        P("dp", "hid", None),
        P("dp", "hid", None),
        P("dp"),
        P("dp"),
        P("dp"),
        P("dp", None, None),
        P("hid", None),
        P("hid", None),
        P("hid", None),
        P("hid", None),
        P("hid", None),
        P("hid", None),
        P(None, "hid"),
        P("hid", None),
        P("dp", None, "hid"),
        P("dp", "hid", None),
    )
    return jax.shard_map(
        shards,
        mesh=mesh,
        in_specs=placed,
        out_specs=(
            P("dp", "hid", None),
            P("dp", "hid", None),
            P("hid", None),
            P("hid", None),
            P("hid", None),
            P("hid", None),
            P("hid", None),
            P("hid", None),
            P(None, "hid"),
            P("hid", None),
            P("dp", None, "hid"),
            P("dp", "hid", None),
        ),
        check_vma=False,
    )
```
